32 devices in a mesh: dp: 8 (over z, y), tensor: 4 (over x, core).
Axes of the slice: x: 2, y: 2, z: 4, core: 2. Of those that a mesh axis runs over, the one named last changes fastest.
Arguments:
- hidden_in: bfloat16 [4096, 1024], P(('dp', 'tensor')), may hold values from -5 to 5
- cotangent: bfloat16 [4096, 1024], P(('dp', 'tensor')), may hold values from -20 to 20
- segments: int32 [8, 512], P('dp'), may hold values from 0 to 3, as said below
- routes: int32 [4096, 8], P(('dp', 'tensor')), may hold values from 0 to 31, as said below
- gain_attn: float32 [1024], replicated, may hold values from 0.5 to 1.5
- w_query: bfloat16 [1024, 1024], P(None, 'tensor'), may hold values from -0.125 to 0.125
- key_matrix: bfloat16 [1024, 512], P(None, 'tensor'), may hold values from -0.125 to 0.125
- value_matrix: bfloat16 [1024, 512], P(None, 'tensor'), may hold values from -0.1875 to 0.1875
- attention_output_weight: bfloat16 [1024, 1024], P('tensor'), may hold values from -0.75 to 0.75
- gain_ffn: float32 [1024], replicated, may hold values from 0.5 to 1.5
- w_router: bfloat16 [1024, 32], replicated, may hold values from -0.34 to 0.34
- w_gate: bfloat16 [2, 1024, 512], P(None, None, 'tensor'), may hold values from -0.1875 to 0.1875
- w_up: bfloat16 [2, 1024, 512], P(None, None, 'tensor'), may hold values from -0.1875 to 0.1875
- w_down: bfloat16 [2, 512, 1024], P(None, 'tensor'), may hold values from -0.75 to 0.75
Outputs:
- output: bfloat16 [4096, 1024], P(('dp', 'tensor'))
- grad_in: float32 [4096, 1024], P(('dp', 'tensor'))
- grad_gain_attn: float32 [1024], replicated
- grad_w_query: float32 [1024, 1024], P(None, 'tensor')
- grad_w_key: float32 [1024, 512], P(None, 'tensor')
- grad_w_value: float32 [1024, 512], P(None, 'tensor')
- grad_w_out: float32 [1024, 1024], P('tensor')
- grad_gain_ffn: float32 [1024], replicated
- grad_router: float32 [1024, 32], replicated
- grad_gate: float32 [2, 1024, 512], P(None, None, 'tensor')
- grad_up: float32 [2, 1024, 512], P(None, None, 'tensor')
- grad_down: float32 [2, 512, 1024], P(None, 'tensor')
The draws below stay inside these ranges and needn't reach their ends.
Inputs may be any that keep to these rules, and one draw needn't show every extreme that they name: `segments`: numbers start at 0 and rise by one at each new document along a packed sequence; a packed sequence holds 2 to 4 documents, each of 102 to 256 tokens. `routes`: each token names 8 different experts.
All inputs are finite; a program needn't handle non-finite values.
Results may differ from the reference program's by a relative error of at most 0.034.
Values may be sent and summed in bfloat16 or wider, within the bound.
A program may use at most 128 MiB of HBM per device.

```python
import jax
import jax.numpy as jnp
from jax import lax

MODEL_WIDTH = 1024
QUERY_HEADS = 16
KEY_VALUE_HEADS = 8
HEAD_SIZE = 64
EXPERTS = 32
TOPK = 8
FF = 512
WIN = 2
DOCS = 4
SEQ = 512
TOKENS = 4096


def projection_drawn(private_key, heads):
    return jax.random.normal(private_key, (MODEL_WIDTH, heads * HEAD_SIZE)) * MODEL_WIDTH ** (-0.5)


def draw_w_query(key, part):
    private_key = jax.random.fold_in(key, 21)
    limit = 4.0 * MODEL_WIDTH ** (-0.5)
    drawn_values = projection_drawn(private_key, QUERY_HEADS)
    return jnp.clip(drawn_values, -limit, limit).astype(jnp.bfloat16)


def draw_key_matrix(key, part):
    private_key = jax.random.fold_in(key, 22)
    limit = 4.0 * MODEL_WIDTH ** (-0.5)
    drawn_values = projection_drawn(private_key, KEY_VALUE_HEADS)
    return jnp.clip(drawn_values, -limit, limit).astype(jnp.bfloat16)


def draw_w_router(key, part):
    private_key = jax.random.fold_in(key, 23)
    spread_scale = 0.7 * MODEL_WIDTH ** (-0.5)
    limit = 0.34
    drawn_values = jax.random.normal(private_key, (MODEL_WIDTH, EXPERTS)) * spread_scale
    return jnp.clip(drawn_values, -limit, limit).astype(jnp.bfloat16)


def draw_hidden_in(key, part):
    private_key = jax.random.fold_in(key, 24)
    drawn_values = jax.random.normal(private_key, (TOKENS, MODEL_WIDTH))
    return jnp.clip(drawn_values, -5.0, 5.0).astype(jnp.bfloat16)


def draw_cotangent(key, part):
    private_key = jax.random.fold_in(key, 25)
    row_index = jnp.arange(TOKENS).astype(jnp.float32)
    rise = jnp.exp(jnp.log(3.0) * row_index / TOKENS)[:, None]
    drawn_values = jnp.clip(jax.random.normal(private_key, (TOKENS, MODEL_WIDTH)), -5.0, 5.0) * rise
    return jnp.clip(drawn_values, -20.0, 20.0).astype(jnp.bfloat16)


def draw_routes(key, part):
    private_key = jax.random.fold_in(key, 27)
    score_key, favour_key = jax.random.split(private_key)
    raw_scores = jax.random.randint(score_key, (TOKENS, EXPERTS), 0, 2 ** 20, dtype=jnp.int32)
    favour_draw = jax.random.randint(favour_key, (TOKENS, EXPERTS), 0, 100, dtype=jnp.int32)
    expert_index = jnp.arange(EXPERTS, dtype=jnp.int32)[None, :]
    favoured = (favour_draw < 78) & (expert_index < WIN)
    scores = raw_scores * EXPERTS + expert_index + jnp.where(favoured, 2 ** 26, 0).astype(jnp.int32)
    picked_vals, picked = lax.top_k(scores, TOPK)
    return picked.astype(jnp.int32)


def draw_segments(key, part):
    private_key = jax.random.fold_in(key, 26)
    rows_count = TOKENS // SEQ
    low_len = SEQ // 5
    high_len = SEQ // 2
    count_key, order_key, length_key = jax.random.split(private_key, 3)
    doc_count = jax.random.randint(count_key, (rows_count,), 2, DOCS + 1)
    order = jax.random.permutation(order_key, rows_count)
    doc_count = jnp.where(order == 0, 2, doc_count)
    doc_count = jnp.where(order == 1, DOCS, doc_count)
    remain = jnp.full((rows_count,), SEQ, jnp.int32)
    cursor = jnp.zeros((rows_count,), jnp.int32)
    position = jnp.arange(SEQ)[None, :]
    seg_vals = jnp.zeros((rows_count, SEQ), jnp.int32)
    for slot in range(DOCS - 1):
        after = doc_count - 1 - slot
        active = after >= 1
        lower = jnp.maximum(low_len, remain - after * high_len)
        upper = jnp.minimum(high_len, remain - after * low_len)
        lower = jnp.where(active, lower, 0)
        upper = jnp.where(active, upper, 0)
        length = jax.random.randint(jax.random.fold_in(length_key, slot), (rows_count,), lower, upper + 1)
        length = jnp.where(active, length, 0)
        cursor = cursor + length
        remain = remain - length
        boundary = jnp.where(active, cursor, SEQ)
        seg_vals = seg_vals + (position >= boundary[:, None]).astype(jnp.int32)
    return seg_vals.astype(jnp.int32)


def shard_levels(rng, shape, cuts, smallest, largest):
    level, own = 1.0, jax.random.fold_in(rng, 6)
    for dim, blocks in cuts:
        draws = jnp.exp(jax.random.uniform(jax.random.fold_in(own, dim), (blocks,), jnp.float32, smallest / len(cuts), largest / len(cuts)))
        level = level * jnp.repeat(draws, shape[dim] // blocks).reshape([-1 if axis == dim else 1 for axis in range(len(shape))])
    return level


def centred(rng, extent, spread, reach, shards=(), held_as=jnp.bfloat16):
    entries = spread * jax.random.normal(rng, extent, jnp.float32)
    if shards:
        entries = entries * shard_levels(rng, extent, shards, -0.22, 0.18)
    return jnp.clip(entries, -reach, reach).astype(held_as)


def setup_inputs(seed: int = 0) -> dict:
    seeds = jax.random.split(jax.random.key(seed), 15)
    return {
        "hidden_in": draw_hidden_in(jax.random.fold_in(seeds[14], 71), 0),
        "cotangent": draw_cotangent(jax.random.fold_in(seeds[14], 71), 0),
        "segments": draw_segments(jax.random.fold_in(seeds[14], 71), 0),
        "routes": draw_routes(jax.random.fold_in(seeds[14], 71), 0),
        "gain_attn": jnp.clip(1.0 + 0.1 * jax.random.normal(seeds[4], (MODEL_WIDTH,), jnp.float32), 0.5, 1.5),
        "w_query": draw_w_query(jax.random.fold_in(seeds[14], 71), 0),
        "key_matrix": draw_key_matrix(jax.random.fold_in(seeds[14], 71), 0),
        "value_matrix": centred(seeds[7], (MODEL_WIDTH, KEY_VALUE_HEADS * HEAD_SIZE), MODEL_WIDTH ** -0.5, 0.1875, ((1, 4),)),
        "attention_output_weight": centred(seeds[8], (QUERY_HEADS * HEAD_SIZE, MODEL_WIDTH), HEAD_SIZE ** -0.5, 0.75, ((0, 4),)),
        "gain_ffn": jnp.clip(1.0 + 0.1 * jax.random.normal(seeds[9], (MODEL_WIDTH,), jnp.float32), 0.5, 1.5),
        "w_router": draw_w_router(jax.random.fold_in(seeds[14], 71), 0),
        "w_gate": centred(seeds[11], (WIN, MODEL_WIDTH, FF), MODEL_WIDTH ** -0.5, 0.1875, ((2, 4),)),
        "w_up": centred(seeds[12], (WIN, MODEL_WIDTH, FF), MODEL_WIDTH ** -0.5, 0.1875, ((2, 4),)),
        "w_down": centred(seeds[13], (WIN, FF, MODEL_WIDTH), (FF // 8) ** -0.5, 0.75, ((1, 4),)),
    }


EPS = 1e-06
THETA = 10000.0
NEGATIVE = -1e+30

def round_trip(array_in):
    return lax.optimization_barrier(array_in.astype(jnp.bfloat16)).astype(jnp.float32)

def inner_rows(left_op, right_op):
    return lax.dot_general(left_op, right_op, (((0,), (0,)), ((), ())), preferred_element_type=jnp.float32)

def outer_columns(left_op, right_op):
    return lax.dot_general(left_op, right_op, (((1,), (1,)), ((), ())), preferred_element_type=jnp.float32)

def rotary_tables(sequence_rows):
    half_dim = HEAD_SIZE // 2
    freq_table = THETA ** (-(jnp.arange(half_dim).astype(jnp.float32) * 2.0 / HEAD_SIZE))
    angles = jnp.arange(sequence_rows).astype(jnp.float32)[:, None] * freq_table[None, :]
    return (jnp.cos(angles)[:, None, :], jnp.sin(angles)[:, None, :])

def apply_rotary(vals_in, cosine_table, sine_values, direction):
    half_dim = vals_in.shape[-1] // 2
    first_half = vals_in[..., :half_dim]
    second_half = vals_in[..., half_dim:]
    return jnp.concatenate([first_half * cosine_table - direction * second_half * sine_values, second_half * cosine_table + direction * first_half * sine_values], axis=-1)

def norm_forward(row_vals, gain_vec):
    inverse = lax.rsqrt(lax.optimization_barrier(jnp.mean(row_vals * row_vals, axis=-1, keepdims=True)) + EPS)
    normed = row_vals * inverse
    return ((normed * gain_vec).astype(jnp.bfloat16), normed, inverse)

def norm_backward(grad_out, normed, inverse, gain_vec):
    grad_gain = lax.optimization_barrier(jnp.sum(grad_out * normed, axis=0))
    scaled = grad_out * gain_vec
    grad_rows = inverse * (scaled - normed * lax.optimization_barrier(jnp.mean(scaled * normed, axis=-1, keepdims=True)))
    return (grad_rows, grad_gain)

def gate_parts(gate_pre):
    sig_vals = jax.nn.sigmoid(gate_pre)
    return (gate_pre * sig_vals, sig_vals * (1.0 + gate_pre * (1.0 - sig_vals)))

def one_sequence(hidden_in, cotangent, seg_row, routes, gain_attn, w_query, key_matrix, value_matrix, attention_output_weight, gain_ffn, w_router, w_gate, w_up, w_down):
    sequence_rows = hidden_in.shape[0]
    query_groups = QUERY_HEADS // KEY_VALUE_HEADS
    scale_factor = HEAD_SIZE ** (-0.5)
    cosine_table, sine_values = rotary_tables(sequence_rows)
    rows_in = hidden_in.astype(jnp.float32)
    attention_normed, unit_attn, inverse_attn = norm_forward(rows_in, gain_attn)
    query_before_rotary = jnp.dot(attention_normed, w_query, preferred_element_type=jnp.float32).reshape(sequence_rows, QUERY_HEADS, HEAD_SIZE)
    key_before_rotary = jnp.dot(attention_normed, key_matrix, preferred_element_type=jnp.float32).reshape(sequence_rows, KEY_VALUE_HEADS, HEAD_SIZE)
    query_rows = apply_rotary(query_before_rotary, cosine_table, sine_values, 1.0).astype(jnp.bfloat16).reshape(sequence_rows, KEY_VALUE_HEADS, query_groups, HEAD_SIZE)
    keys_rot = apply_rotary(key_before_rotary, cosine_table, sine_values, 1.0).astype(jnp.bfloat16)
    value_inputs = jnp.dot(attention_normed, value_matrix, preferred_element_type=jnp.float32).astype(jnp.bfloat16).reshape(sequence_rows, KEY_VALUE_HEADS, HEAD_SIZE)
    positions = jnp.arange(sequence_rows)
    allowed = (seg_row[:, None] == seg_row[None, :]) & (positions[None, :] <= positions[:, None])
    scores = jnp.einsum('qhgd,khd->hgqk', query_rows.astype(jnp.float32), keys_rot.astype(jnp.float32)) * scale_factor
    scores = jnp.where(allowed[None, None], scores, NEGATIVE)
    peak_score = lax.optimization_barrier(jnp.max(scores, axis=-1, keepdims=True))
    log_total = peak_score + jnp.log(lax.optimization_barrier(jnp.sum(jnp.exp(scores - peak_score), axis=-1, keepdims=True)))
    probs_all = jnp.exp(scores - log_total)
    probs_bf = round_trip(probs_all)
    mixed_heads = jnp.einsum('hgqk,khd->qhgd', probs_bf, value_inputs.astype(jnp.float32)).astype(jnp.bfloat16)
    mixed_flat = mixed_heads.reshape(sequence_rows, QUERY_HEADS * HEAD_SIZE)
    attn_out = jnp.dot(mixed_flat, attention_output_weight, preferred_element_type=jnp.float32)
    after_attn = rows_in + attn_out
    normed_ffn, unit_ffn, inverse_ffn = norm_forward(after_attn, gain_ffn)
    router_logits = jnp.dot(normed_ffn, w_router, preferred_element_type=jnp.float32)
    router_probs = jax.nn.softmax(router_logits, axis=-1)
    chosen_probs = jnp.take_along_axis(router_probs, routes, axis=1)
    picked_mask = (routes[:, :, None] == jnp.arange(WIN)[None, None, :]).astype(jnp.float32)
    combine_used = round_trip(lax.optimization_barrier(jnp.sum(chosen_probs[:, :, None] * picked_mask, axis=1)))
    combined = jnp.zeros((sequence_rows, MODEL_WIDTH), jnp.float32)
    saved_parts = []
    for expert in range(WIN):
        gate_pre = jnp.dot(normed_ffn, w_gate[expert], preferred_element_type=jnp.float32)
        up_pre = jnp.dot(normed_ffn, w_up[expert], preferred_element_type=jnp.float32)
        silu_val, slope_val = gate_parts(gate_pre)
        inner_act = (silu_val * up_pre).astype(jnp.bfloat16)
        expert_out = jnp.dot(inner_act, w_down[expert], preferred_element_type=jnp.float32)
        combined = combined + combine_used[:, expert:expert + 1] * expert_out
        saved_parts.append((up_pre, silu_val, slope_val, inner_act, expert_out))
    output = (after_attn + combined).astype(jnp.bfloat16)
    grad_top = cotangent.astype(jnp.float32)
    grad_normed_ffn = jnp.zeros((sequence_rows, MODEL_WIDTH), jnp.float32)
    grad_combine_list, grad_gate_list, grad_up_list, grad_down_list = ([], [], [], [])
    for expert in range(WIN):
        up_pre, silu_val, slope_val, inner_act, expert_out = saved_parts[expert]
        grad_expert = (combine_used[:, expert:expert + 1] * grad_top).astype(jnp.bfloat16)
        grad_combine_list.append(lax.optimization_barrier(jnp.sum(grad_top * expert_out, axis=-1)))
        grad_down_list.append(inner_rows(inner_act, grad_expert))
        grad_inner = outer_columns(grad_expert, w_down[expert])
        grad_gate_pre = (grad_inner * up_pre * slope_val).astype(jnp.bfloat16)
        grad_up_pre = (grad_inner * silu_val).astype(jnp.bfloat16)
        grad_gate_list.append(inner_rows(normed_ffn, grad_gate_pre))
        grad_up_list.append(inner_rows(normed_ffn, grad_up_pre))
        grad_normed_ffn = grad_normed_ffn + outer_columns(grad_gate_pre, w_gate[expert]) + outer_columns(grad_up_pre, w_up[expert])
    grad_combine = jnp.stack(grad_combine_list, axis=1)
    route_counts = lax.optimization_barrier(jnp.sum(picked_mask, axis=1))
    grad_rprobs = jnp.concatenate([grad_combine * route_counts, jnp.zeros((sequence_rows, EXPERTS - WIN), jnp.float32)], axis=1)
    grad_logits = (router_probs * (grad_rprobs - lax.optimization_barrier(jnp.sum(router_probs * grad_rprobs, axis=-1, keepdims=True)))).astype(jnp.bfloat16)
    grad_router = inner_rows(normed_ffn, grad_logits)
    grad_normed_ffn = grad_normed_ffn + outer_columns(grad_logits, w_router)
    grad_after, grad_gain_ffn = norm_backward(grad_normed_ffn, unit_ffn, inverse_ffn, gain_ffn)
    grad_after = grad_after + grad_top
    gradient_after_half = grad_after.astype(jnp.bfloat16)
    grad_w_out = inner_rows(mixed_flat, gradient_after_half)
    mixed_gradient = outer_columns(gradient_after_half, attention_output_weight).astype(jnp.bfloat16).reshape(sequence_rows, KEY_VALUE_HEADS, query_groups, HEAD_SIZE)
    grad_mixed32 = mixed_gradient.astype(jnp.float32)
    delta_rows = jnp.transpose(lax.optimization_barrier(jnp.sum(grad_mixed32 * mixed_heads.astype(jnp.float32), axis=-1)), (1, 2, 0))[..., None]
    value_gradients = jnp.einsum('hgqk,qhgd->khd', probs_bf, grad_mixed32)
    grad_probs = jnp.einsum('qhgd,khd->hgqk', grad_mixed32, value_inputs.astype(jnp.float32))
    grad_scores = round_trip(probs_all * (grad_probs - delta_rows) * scale_factor)
    grad_query = jnp.einsum('hgqk,khd->qhgd', grad_scores, keys_rot.astype(jnp.float32))
    key_gradient = jnp.einsum('hgqk,qhgd->khd', grad_scores, query_rows.astype(jnp.float32))
    grad_query_bf = apply_rotary(grad_query.reshape(sequence_rows, QUERY_HEADS, HEAD_SIZE), cosine_table, sine_values, -1.0).astype(jnp.bfloat16).reshape(sequence_rows, QUERY_HEADS * HEAD_SIZE)
    key_gradient_half = apply_rotary(key_gradient, cosine_table, sine_values, -1.0).astype(jnp.bfloat16).reshape(sequence_rows, KEY_VALUE_HEADS * HEAD_SIZE)
    value_gradient_half = value_gradients.astype(jnp.bfloat16).reshape(sequence_rows, KEY_VALUE_HEADS * HEAD_SIZE)
    grad_w_query = inner_rows(attention_normed, grad_query_bf)
    grad_w_key = inner_rows(attention_normed, key_gradient_half)
    grad_w_value = inner_rows(attention_normed, value_gradient_half)
    grad_normed_attn = outer_columns(grad_query_bf, w_query) + outer_columns(key_gradient_half, key_matrix) + outer_columns(value_gradient_half, value_matrix)
    grad_in, grad_gain_attn = norm_backward(grad_normed_attn, unit_attn, inverse_attn, gain_attn)
    grad_in = grad_in + grad_after
    grads = (grad_gain_attn, grad_w_query, grad_w_key, grad_w_value, grad_w_out, grad_gain_ffn, grad_router, jnp.stack(grad_gate_list), jnp.stack(grad_up_list), jnp.stack(grad_down_list))
    return (output, grad_in, grads)

def reference(hidden_in, cotangent, segments, routes, gain_attn, w_query, key_matrix, value_matrix, attention_output_weight, gain_ffn, w_router, w_gate, w_up, w_down):
    seq_count = hidden_in.shape[0] // SEQ
    rows_seq = hidden_in.reshape(seq_count, SEQ, MODEL_WIDTH)
    cot_seq = cotangent.reshape(seq_count, SEQ, MODEL_WIDTH)
    route_seq = routes.reshape(seq_count, SEQ, TOPK)
    zero_grads = (jnp.zeros(gain_attn.shape, jnp.float32), jnp.zeros(w_query.shape, jnp.float32), jnp.zeros(key_matrix.shape, jnp.float32), jnp.zeros(value_matrix.shape, jnp.float32), jnp.zeros(attention_output_weight.shape, jnp.float32), jnp.zeros(gain_ffn.shape, jnp.float32), jnp.zeros(w_router.shape, jnp.float32), jnp.zeros(w_gate.shape, jnp.float32), jnp.zeros(w_up.shape, jnp.float32), jnp.zeros(w_down.shape, jnp.float32))

    def step_fn(carry, items):
        output, grad_in, grads = one_sequence(items[0], items[1], items[2], items[3], gain_attn, w_query, key_matrix, value_matrix, attention_output_weight, gain_ffn, w_router, w_gate, w_up, w_down)
        return (tuple((old + new for old, new in zip(carry, grads))), (output, grad_in))
    totals, stacked = lax.scan(step_fn, zero_grads, (rows_seq, cot_seq, segments, route_seq))
    output = stacked[0].reshape(seq_count * SEQ, MODEL_WIDTH)
    grad_in = stacked[1].reshape(seq_count * SEQ, MODEL_WIDTH)
    return (output, grad_in, totals[0], totals[1], totals[2], totals[3], totals[4], totals[5], totals[6], totals[7], totals[8], totals[9])
```

```python
import jax
import jax.numpy as jnp
from jax import lax
from jax.sharding import PartitionSpec as P

HEAD_SIZE = 64


EPS = 1e-06
THETA = 10000.0
NEGATIVE = -1e30


def inner_rows(left_op, right_op):
    return lax.dot_general(
        left_op, right_op, (((0,), (0,)), ((), ())), preferred_element_type=jnp.float32
    )


def outer_columns(left_op, right_op):
    return lax.dot_general(
        left_op, right_op, (((1,), (1,)), ((), ())), preferred_element_type=jnp.float32
    )


def rotary_tables(sequence_rows):
    half_dim = HEAD_SIZE // 2
    freq_table = THETA ** (-(jnp.arange(half_dim).astype(jnp.float32) * 2.0 / HEAD_SIZE))
    angles = jnp.arange(sequence_rows).astype(jnp.float32)[:, None] * freq_table[None, :]
    return (jnp.cos(angles)[:, None, :], jnp.sin(angles)[:, None, :])


def apply_rotary(vals_in, cosine_table, sine_values, direction):
    half_dim = vals_in.shape[-1] // 2
    first_half = vals_in[..., :half_dim]
    second_half = vals_in[..., half_dim:]
    return jnp.concatenate(
        [
            first_half * cosine_table - direction * second_half * sine_values,
            second_half * cosine_table + direction * first_half * sine_values,
        ],
        axis=-1,
    )


def norm_forward(row_vals, gain_vec):
    inverse = lax.rsqrt(jnp.mean(row_vals * row_vals, axis=-1, keepdims=True) + EPS)
    normed = row_vals * inverse
    return ((normed * gain_vec).astype(jnp.bfloat16), normed, inverse)


def norm_backward(grad_out, normed, inverse, gain_vec):
    grad_gain = jnp.sum(grad_out * normed, axis=0)
    scaled = grad_out * gain_vec
    grad_rows = inverse * (scaled - normed * jnp.mean(scaled * normed, axis=-1, keepdims=True))
    return (grad_rows, grad_gain)


def gate_parts(gate_pre):
    sig_vals = jax.nn.sigmoid(gate_pre)
    return (gate_pre * sig_vals, sig_vals * (1.0 + gate_pre * (1.0 - sig_vals)))


def beside(left, right):
    pad = jnp.zeros((right.shape[0], 128 - right.shape[1]), left.dtype)
    return jnp.concatenate([left, right.astype(left.dtype), pad], axis=1)


def scatter_sum(part):
    return lax.psum_scatter(
        part.astype(jnp.bfloat16), "tensor", scatter_dimension=0, tiled=True
    ).astype(jnp.float32)


def block_scores(query_block, keys_part, seg_row, row_start, row_stop):
    allowed = (seg_row[row_start:row_stop, None] == seg_row[None, :row_stop]) & (
        jnp.arange(row_stop)[None, :] <= jnp.arange(row_start, row_stop)[:, None]
    )
    scores = jnp.einsum(
        "qhgd,khd->hgqk", query_block, keys_part, preferred_element_type=jnp.float32
    ) * HEAD_SIZE ** (-0.5)
    return jnp.where(allowed[None, None], scores, NEGATIVE)


def on_device(
    hidden_in,
    cotangent,
    segments,
    routes,
    gain_attn,
    w_query,
    key_matrix,
    value_matrix,
    attention_output_weight,
    gain_ffn,
    w_router,
    w_gate,
    w_up,
    w_down,
):
    shard_rows = hidden_in.shape[0]
    width = hidden_in.shape[1]
    seg_row = segments[0]
    sequence_rows = seg_row.shape[0]
    kv_local = key_matrix.shape[1] // HEAD_SIZE
    heads_local = w_query.shape[1] // HEAD_SIZE
    query_groups = heads_local // kv_local
    experts_win = w_gate.shape[0]
    block_rows = min(512, sequence_rows)
    scale_factor = HEAD_SIZE ** (-0.5)
    cosine_table, sine_values = rotary_tables(sequence_rows)
    rows_in = hidden_in.astype(jnp.float32)
    attention_normed, unit_attn, inverse_attn = norm_forward(rows_in, gain_attn)
    gathered = lax.all_gather(
        jnp.concatenate([attention_normed, cotangent], axis=1), "tensor", axis=0, tiled=True
    )
    full_attn = gathered[:, :width]
    grad_full = gathered[:, width:]
    query_before_rotary = jnp.dot(full_attn, w_query, preferred_element_type=jnp.float32).reshape(
        sequence_rows, heads_local, HEAD_SIZE
    )
    key_before_rotary = jnp.dot(full_attn, key_matrix, preferred_element_type=jnp.float32).reshape(
        sequence_rows, kv_local, HEAD_SIZE
    )
    query_rows = (
        apply_rotary(query_before_rotary, cosine_table, sine_values, 1.0)
        .astype(jnp.bfloat16)
        .reshape(sequence_rows, kv_local, query_groups, HEAD_SIZE)
    )
    keys_rot = apply_rotary(key_before_rotary, cosine_table, sine_values, 1.0).astype(jnp.bfloat16)
    value_inputs = (
        jnp.dot(full_attn, value_matrix, preferred_element_type=jnp.float32)
        .astype(jnp.bfloat16)
        .reshape(sequence_rows, kv_local, HEAD_SIZE)
    )
    row_start = 0
    row_stop = row_start + block_rows
    scores = block_scores(query_rows, keys_rot, seg_row, row_start, row_stop)
    peak_score = jnp.max(scores, axis=-1, keepdims=True)
    log_total = peak_score + jnp.log(jnp.sum(jnp.exp(scores - peak_score), axis=-1, keepdims=True))
    probs_blk = jnp.exp(scores - log_total)
    mixed_parts = jnp.einsum(
        "hgqk,khd->qhgd",
        probs_blk.astype(jnp.bfloat16),
        value_inputs,
        preferred_element_type=jnp.float32,
    ).astype(jnp.bfloat16)
    log_totals = [log_total]
    mixed_flat = mixed_parts.reshape(sequence_rows, heads_local * HEAD_SIZE)
    attn_out = scatter_sum(
        jnp.dot(mixed_flat, attention_output_weight, preferred_element_type=jnp.float32)
    )
    after_attn = rows_in + attn_out
    normed_ffn, unit_ffn, inverse_ffn = norm_forward(after_attn, gain_ffn)
    router_logits = jnp.dot(normed_ffn, w_router, preferred_element_type=jnp.float32)
    router_probs = jax.nn.softmax(router_logits, axis=-1)
    picked_mask = (routes[:, :, None] == jnp.arange(experts_win)[None, None, :]).astype(jnp.float32)
    route_counts = jnp.sum(picked_mask, axis=1)
    combine_bf = (router_probs[:, :experts_win] * route_counts).astype(jnp.bfloat16)
    gathered_ffn = lax.all_gather(beside(normed_ffn, combine_bf), "tensor", axis=0, tiled=True)
    full_ffn = gathered_ffn[:, :width]
    full_combine = gathered_ffn[:, width : width + experts_win]
    combine_used = full_combine.astype(jnp.float32)
    combined = jnp.zeros((sequence_rows, width), jnp.float32)
    saved_parts = []
    for expert in range(experts_win):
        gate_pre = jnp.dot(full_ffn, w_gate[expert], preferred_element_type=jnp.float32)
        up_pre = jnp.dot(full_ffn, w_up[expert], preferred_element_type=jnp.float32)
        silu_val, slope_val = gate_parts(gate_pre)
        inner_act = (silu_val * up_pre).astype(jnp.bfloat16)
        expert_out = jnp.dot(inner_act, w_down[expert], preferred_element_type=jnp.float32)
        combined = combined + combine_used[:, expert : expert + 1] * expert_out
        saved_parts.append((up_pre, silu_val, slope_val, inner_act, expert_out))
    combined = combined.astype(jnp.bfloat16)
    grad_full32 = grad_full.astype(jnp.float32)
    partial_rows = jnp.zeros((sequence_rows, width), jnp.float32)
    grad_combine_list, grad_gate_list, grad_up_list, grad_down_list = ([], [], [], [])
    for expert in range(experts_win):
        up_pre, silu_val, slope_val, inner_act, expert_out = saved_parts[expert]
        grad_expert = (combine_used[:, expert : expert + 1] * grad_full32).astype(jnp.bfloat16)
        grad_combine_list.append(jnp.sum(grad_full32 * expert_out, axis=-1))
        grad_down_list.append(inner_rows(inner_act, grad_expert))
        grad_inner = outer_columns(grad_expert, w_down[expert])
        grad_gate_pre = (grad_inner * up_pre * slope_val).astype(jnp.bfloat16)
        grad_up_pre = (grad_inner * silu_val).astype(jnp.bfloat16)
        grad_gate_list.append(grad_gate_pre)
        grad_up_list.append(grad_up_pre)
        partial_rows = (
            partial_rows
            + outer_columns(grad_gate_pre, w_gate[expert])
            + outer_columns(grad_up_pre, w_up[expert])
        )
    grad_combine_part = jnp.stack(grad_combine_list, axis=1)
    scattered = scatter_sum(beside(partial_rows.astype(jnp.bfloat16), grad_combine_part))
    grad_normed_part = scattered[:, :width]
    grad_combine = scattered[:, width : width + experts_win]
    grad_down = jnp.concatenate(grad_down_list, axis=0)
    grad_rprobs = jnp.concatenate(
        [
            grad_combine * route_counts,
            jnp.zeros((shard_rows, w_router.shape[1] - experts_win), jnp.float32),
        ],
        axis=1,
    )
    grad_logits = (
        router_probs * (grad_rprobs - jnp.sum(router_probs * grad_rprobs, axis=-1, keepdims=True))
    ).astype(jnp.bfloat16)
    grad_normed_ffn = grad_normed_part + outer_columns(grad_logits, w_router)
    grad_after, grad_gain_ffn = norm_backward(grad_normed_ffn, unit_ffn, inverse_ffn, gain_ffn)
    grad_after = grad_after + cotangent.astype(jnp.float32)
    gathered_after = lax.all_gather(
        beside(grad_after.astype(jnp.bfloat16), grad_logits), "tensor", axis=0, tiled=True
    )
    full_grad_after = gathered_after[:, :width]
    full_logits = gathered_after[:, width:]
    ffn_sums = inner_rows(
        full_ffn, jnp.concatenate(grad_gate_list + grad_up_list + [full_logits], axis=1)
    ).astype(jnp.bfloat16)
    grad_w_out = inner_rows(mixed_flat, full_grad_after)
    mixed_gradient = (
        outer_columns(full_grad_after, attention_output_weight)
        .astype(jnp.bfloat16)
        .reshape(sequence_rows, kv_local, query_groups, HEAD_SIZE)
    )
    delta_rows = jnp.transpose(
        jnp.sum(mixed_gradient.astype(jnp.float32) * mixed_parts.astype(jnp.float32), axis=-1),
        (1, 2, 0),
    )[..., None]
    grad_keys = jnp.zeros((sequence_rows, kv_local, HEAD_SIZE), jnp.float32)
    value_gradients = jnp.zeros((sequence_rows, kv_local, HEAD_SIZE), jnp.float32)
    grad_query_parts = []
    for block_index, row_start in enumerate(range(0, sequence_rows, block_rows)):
        row_stop = row_start + block_rows
        scores = block_scores(query_rows, keys_rot, seg_row, row_start, row_stop)
        probs_blk = jnp.exp(scores - log_totals[block_index])
        value_gradients = value_gradients.at[:row_stop].add(
            jnp.einsum(
                "hgqk,qhgd->khd",
                probs_blk.astype(jnp.bfloat16),
                mixed_gradient,
                preferred_element_type=jnp.float32,
            )
        )
        grad_probs = jnp.einsum(
            "qhgd,khd->hgqk", mixed_gradient, value_inputs, preferred_element_type=jnp.float32
        )
        grad_scores = (probs_blk * (grad_probs - delta_rows) * scale_factor).astype(jnp.bfloat16)
        grad_query_parts.append(
            jnp.einsum("hgqk,khd->qhgd", grad_scores, keys_rot, preferred_element_type=jnp.float32)
        )
        grad_keys = grad_keys.at[:row_stop].add(
            jnp.einsum(
                "hgqk,qhgd->khd", grad_scores, query_rows, preferred_element_type=jnp.float32
            )
        )
    grad_query = grad_query_parts[0].reshape(sequence_rows, heads_local, HEAD_SIZE)
    grad_query_bf = (
        apply_rotary(grad_query, cosine_table, sine_values, -1.0)
        .astype(jnp.bfloat16)
        .reshape(sequence_rows, heads_local * HEAD_SIZE)
    )
    key_gradient_half = (
        apply_rotary(grad_keys, cosine_table, sine_values, -1.0)
        .astype(jnp.bfloat16)
        .reshape(sequence_rows, kv_local * HEAD_SIZE)
    )
    value_gradient_half = value_gradients.astype(jnp.bfloat16).reshape(
        sequence_rows, kv_local * HEAD_SIZE
    )
    attn_sums = inner_rows(
        full_attn,
        jnp.concatenate([grad_query_bf, key_gradient_half, value_gradient_half], axis=1),
    ).astype(jnp.bfloat16)
    row_sums = jnp.concatenate([grad_down, grad_w_out], axis=0).astype(jnp.bfloat16)
    grad_normed_attn = scatter_sum(
        outer_columns(grad_query_bf, w_query)
        + outer_columns(key_gradient_half, key_matrix)
        + outer_columns(value_gradient_half, value_matrix)
    )
    grad_normed_attn, combined = lax.optimization_barrier((grad_normed_attn, combined))
    output = (after_attn + scatter_sum(combined)).astype(jnp.bfloat16)
    grad_in, grad_gain_attn = norm_backward(grad_normed_attn, unit_attn, inverse_attn, gain_attn)
    grad_in = grad_in + grad_after
    gains = jnp.concatenate([grad_gain_ffn, grad_gain_attn]).reshape(-1, 128)
    gains = lax.psum(gains, ("dp", "tensor"))
    ffn_sums, row_sums, attn_sums = lax.psum((ffn_sums, row_sums, attn_sums), "dp")
    ffn_sums = ffn_sums.astype(jnp.float32)
    row_sums = row_sums.astype(jnp.float32)
    attn_sums = attn_sums.astype(jnp.float32)
    hidden = w_gate.shape[2]
    grad_gate = jnp.stack([ffn_sums[:, e * hidden : (e + 1) * hidden] for e in range(experts_win)])
    grad_up = jnp.stack(
        [ffn_sums[:, e * hidden : (e + 1) * hidden] for e in range(experts_win, 2 * experts_win)]
    )
    grad_router = ffn_sums[:, 2 * experts_win * hidden :]
    query_cols = w_query.shape[1]
    key_cols = key_matrix.shape[1]
    grad_w_query = attn_sums[:, :query_cols]
    grad_w_key = attn_sums[:, query_cols : query_cols + key_cols]
    grad_w_value = attn_sums[:, query_cols + key_cols :]
    down_rows = grad_down.shape[0]
    grad_down = row_sums[:down_rows]
    grad_w_out = row_sums[down_rows:]
    gains = gains.reshape(2, width)
    grad_gain_ffn, grad_gain_attn = gains[0], gains[1]
    grad_router = grad_router[:, : w_router.shape[1]]
    grad_down = grad_down.reshape(w_down.shape)
    return (
        output,
        grad_in,
        grad_gain_attn,
        grad_w_query,
        grad_w_key,
        grad_w_value,
        grad_w_out,
        grad_gain_ffn,
        grad_router,
        grad_gate,
        grad_up,
        grad_down,
    )


def solution(mesh):
    return jax.shard_map(
        on_device,
        mesh=mesh,
        in_specs=(
            P(("dp", "tensor"), None),
            P(("dp", "tensor"), None),
            P("dp", None),
            P(("dp", "tensor"), None),
            P(),
            P(None, "tensor"),
            P(None, "tensor"),
            P(None, "tensor"),
            P("tensor", None),
            P(),
            P(),
            P(None, None, "tensor"),
            P(None, None, "tensor"),
            P(None, "tensor", None),
        ),
        out_specs=(
            P(("dp", "tensor"), None),
            P(("dp", "tensor"), None),
            P(),
            P(None, "tensor"),
            P(None, "tensor"),
            P(None, "tensor"),
            P("tensor", None),
            P(),
            P(),
            P(None, None, "tensor"),
            P(None, None, "tensor"),
            P(None, "tensor", None),
        ),
        check_vma=False,
    )
```

```python
import functools
import math

import jax
import jax.numpy as jnp
from jax import lax
from jax.experimental import pallas as pl
from jax.experimental.pallas import tpu as pltpu
from jax.sharding import PartitionSpec as P

HEAD_SIZE = 64


EPS = 1e-06
THETA = 10000.0
NEGATIVE = -1e30


def inner_rows(left_op, right_op):
    return lax.dot_general(
        left_op, right_op, (((0,), (0,)), ((), ())), preferred_element_type=jnp.float32
    )


def outer_columns(left_op, right_op):
    return lax.dot_general(
        left_op, right_op, (((1,), (1,)), ((), ())), preferred_element_type=jnp.float32
    )


def rotary_tables(sequence_rows):
    half_dim = HEAD_SIZE // 2
    freq_table = THETA ** (-(jnp.arange(half_dim).astype(jnp.float32) * 2.0 / HEAD_SIZE))
    angles = jnp.arange(sequence_rows).astype(jnp.float32)[:, None] * freq_table[None, :]
    return (jnp.cos(angles)[:, None, :], jnp.sin(angles)[:, None, :])


def apply_rotary(vals_in, cosine_table, sine_values, direction):
    half_dim = vals_in.shape[-1] // 2
    first_half = vals_in[..., :half_dim]
    second_half = vals_in[..., half_dim:]
    return jnp.concatenate(
        [
            first_half * cosine_table - direction * second_half * sine_values,
            second_half * cosine_table + direction * first_half * sine_values,
        ],
        axis=-1,
    )


def norm_forward(row_vals, gain_vec):
    inverse = lax.rsqrt(jnp.mean(row_vals * row_vals, axis=-1, keepdims=True) + EPS)
    normed = row_vals * inverse
    return ((normed * gain_vec).astype(jnp.bfloat16), normed, inverse)


def norm_backward(grad_out, normed, inverse, gain_vec):
    grad_gain = jnp.sum(grad_out * normed, axis=0)
    scaled = grad_out * gain_vec
    grad_rows = inverse * (scaled - normed * jnp.mean(scaled * normed, axis=-1, keepdims=True))
    return (grad_rows, grad_gain)


def gate_parts(gate_pre):
    sig_vals = jax.nn.sigmoid(gate_pre)
    return (gate_pre * sig_vals, sig_vals * (1.0 + gate_pre * (1.0 - sig_vals)))


def beside(left, right):
    pad = jnp.zeros((right.shape[0], 128 - right.shape[1]), left.dtype)
    return jnp.concatenate([left, right.astype(left.dtype), pad], axis=1)


def scatter_sum(part):
    return lax.psum_scatter(
        part.astype(jnp.bfloat16), "tensor", scatter_dimension=0, tiled=True
    ).astype(jnp.float32)


def block_scores(query_block, keys_part, seg_row, row_start, row_stop):
    allowed = (seg_row[row_start:row_stop, None] == seg_row[None, :row_stop]) & (
        jnp.arange(row_stop)[None, :] <= jnp.arange(row_start, row_stop)[:, None]
    )
    scores = jnp.einsum(
        "qhgd,khd->hgqk", query_block, keys_part, preferred_element_type=jnp.float32
    ) * HEAD_SIZE ** (-0.5)
    return jnp.where(allowed[None, None], scores, NEGATIVE)


MESH = pl.DeviceIdType.MESH


def reduce_kernel(n, inner, tensor_size, *refs):
    outer = n // inner
    pieces, gain_ref = refs[0:3], refs[3]
    gate_out, up_out, router_out, down_out, wo_out, wq_out, wk_out, wv_out, gain_out = refs[4:13]
    first, held, second, full = refs[13:16], refs[16:19], refs[19:22], refs[22:25]
    gain_t, gain_sum, gain_d = refs[25:28]
    send1, recv1, send2, recv2, send3, recv3, send4, recv4 = refs[28:36]
    gsend_t, grecv_t, gsend_d, grecv_d = refs[36:40]
    me = lax.axis_index("dp")
    mt = lax.axis_index("tensor")
    y = me % inner
    z = me // inner

    def remote(src, dst, send, recv, dp_index, tensor_index):
        copy = pltpu.make_async_remote_copy(
            src_ref=src,
            dst_ref=dst,
            send_sem=send,
            recv_sem=recv,
            device_id=(dp_index, tensor_index),
            device_id_type=MESH,
        )
        copy.start()
        return copy

    barrier = pltpu.get_barrier_semaphore()
    for k in range(1, n):
        pl.semaphore_signal(barrier, inc=1, device_id=((me + k) % n, mt), device_id_type=MESH)
    for k in range(1, tensor_size):
        pl.semaphore_signal(
            barrier, inc=1, device_id=(me, (mt + k) % tensor_size), device_id_type=MESH
        )
    pl.semaphore_wait(barrier, n - 1 + tensor_size - 1)

    gain_copies = [
        remote(
            gain_ref, gain_t.at[k - 1], gsend_t.at[k - 1], grecv_t.at[k - 1],
            me, (mt + k) % tensor_size,
        )
        for k in range(1, tensor_size)
    ]
    copies1 = []
    for p in range(3):
        started = []
        for k in range(1, inner):
            to = (y + k) % inner
            started.append(
                remote(
                    pieces[p].at[to], first[p].at[k - 1], send1.at[p, k - 1], recv1.at[p, k - 1],
                    z * inner + to, mt,
                )
            )
        copies1.append(started)
    for copy in gain_copies:
        copy.wait()
    total = gain_ref[...]
    for k in range(1, tensor_size):
        total = total + gain_t[k - 1]
    gain_sum[...] = total
    gain_copies = [
        remote(
            gain_sum, gain_d.at[k - 1], gsend_d.at[k - 1], grecv_d.at[k - 1], (me + k) % n, mt
        )
        for k in range(1, n)
    ]
    copies2 = []
    for p in range(3):
        for copy in copies1[p]:
            copy.wait()
        for o in range(outer):
            acc = pieces[p][y, o].astype(jnp.float32)
            for k in range(1, inner):
                acc = acc + first[p][k - 1, o].astype(jnp.float32)
            held[p][o] = acc.astype(jnp.bfloat16)
        started = []
        for k in range(1, outer):
            to = (z + k) % outer
            started.append(
                remote(
                    held[p].at[to], second[p].at[k - 1], send2.at[p, k - 1], recv2.at[p, k - 1],
                    to * inner + y, mt,
                )
            )
        copies2.append(started)
    copies3 = []
    for p in range(3):
        for copy in copies2[p]:
            copy.wait()
        acc = held[p][z].astype(jnp.float32)
        for k in range(1, outer):
            acc = acc + second[p][k - 1].astype(jnp.float32)
        full[p][y, z] = acc.astype(jnp.bfloat16)
        started = []
        for k in range(1, outer):
            started.append(
                remote(
                    full[p].at[y, z], full[p].at[y, z], send3.at[p, k - 1], recv3.at[p, k - 1],
                    ((z + k) % outer) * inner + y, mt,
                )
            )
        copies3.append(started)
    copies4 = []
    for p in range(3):
        for copy in copies3[p]:
            copy.wait()
        started = []
        for k in range(1, inner):
            started.append(
                remote(
                    full[p].at[y], full[p].at[y], send4.at[p, k - 1], recv4.at[p, k - 1],
                    z * inner + (y + k) % inner, mt,
                )
            )
        copies4.append(started)
    for copy in gain_copies:
        copy.wait()
    total = gain_sum[...]
    for k in range(1, n):
        total = total + gain_d[k - 1]
    gain_out[...] = total

    experts, _, hidden = gate_out.shape
    down_rows = down_out.shape[0]
    query_cols, key_cols = wq_out.shape[1], wk_out.shape[1]
    for p in range(3):
        for copy in copies4[p]:
            copy.wait()
        depth = full[p].shape[2]
        for i in range(inner):
            for o in range(outer):
                block = full[p][i, o].astype(jnp.float32)
                start = (i * outer + o) * depth
                rows = slice(start, start + depth)
                if p == 0:
                    for e in range(experts):
                        gate_out[e, rows, :] = block[:, e * hidden : (e + 1) * hidden]
                        at = (experts + e) * hidden
                        up_out[e, rows, :] = block[:, at : at + hidden]
                    router_out[rows, :] = block[:, 2 * experts * hidden :]
                elif p == 1:
                    if start < down_rows:
                        down_out[rows, :] = block
                    else:
                        wo_out[start - down_rows : start - down_rows + depth, :] = block
                else:
                    wq_out[rows, :] = block[:, :query_cols]
                    wk_out[rows, :] = block[:, query_cols : query_cols + key_cols]
                    wv_out[rows, :] = block[:, query_cols + key_cols :]


def reduce_sums(ffn_sums, row_sums, attn_sums, gains, gate_shape, down_shape, query_shape, key_shape):
    n = lax.axis_size("dp")
    tensor_size = lax.axis_size("tensor")
    inner = math.isqrt(n)
    outer = n // inner
    pieces = [
        piece.reshape(inner, outer, piece.shape[0] // n, piece.shape[1])
        for piece in (ffn_sums, row_sums, attn_sums)
    ]
    blocks = [piece.shape[2:] for piece in pieces]
    down_rows = down_shape[0] * down_shape[1]
    float_out = functools.partial(jax.ShapeDtypeStruct, dtype=jnp.float32)
    out_shape = [
        float_out(gate_shape),
        float_out(gate_shape),
        float_out((ffn_sums.shape[0], 128)),
        float_out((down_rows, row_sums.shape[1])),
        float_out((row_sums.shape[0] - down_rows, row_sums.shape[1])),
        float_out(query_shape),
        float_out(key_shape),
        float_out(key_shape),
        float_out(gains.shape),
    ]
    half = jnp.bfloat16
    scratch = (
        [pltpu.VMEM((inner - 1, outer) + block, half) for block in blocks]
        + [pltpu.VMEM((outer,) + block, half) for block in blocks]
        + [pltpu.VMEM((outer - 1,) + block, half) for block in blocks]
        + [pltpu.VMEM((inner, outer) + block, half) for block in blocks]
        + [
            pltpu.VMEM((tensor_size - 1,) + gains.shape, jnp.float32),
            pltpu.VMEM(gains.shape, jnp.float32),
            pltpu.VMEM((n - 1,) + gains.shape, jnp.float32),
        ]
        + [pltpu.SemaphoreType.DMA((3, inner - 1))] * 2
        + [pltpu.SemaphoreType.DMA((3, outer - 1))] * 4
        + [pltpu.SemaphoreType.DMA((3, inner - 1))] * 2
        + [pltpu.SemaphoreType.DMA((tensor_size - 1,))] * 2
        + [pltpu.SemaphoreType.DMA((n - 1,))] * 2
    )
    vmem = pl.BlockSpec(memory_space=pltpu.VMEM)
    return pl.pallas_call(
        functools.partial(reduce_kernel, n, inner, tensor_size),
        out_shape=out_shape,
        in_specs=[vmem] * 4,
        out_specs=[vmem] * 9,
        scratch_shapes=scratch,
        compiler_params=pltpu.CompilerParams(
            collective_id=0, has_side_effects=True, vmem_limit_bytes=48 * 1024 * 1024
        ),
    )(*pieces, gains)


def on_device(
    hidden_in,
    cotangent,
    segments,
    routes,
    gain_attn,
    w_query,
    key_matrix,
    value_matrix,
    attention_output_weight,
    gain_ffn,
    w_router,
    w_gate,
    w_up,
    w_down,
):
    shard_rows = hidden_in.shape[0]
    width = hidden_in.shape[1]
    seg_row = segments[0]
    sequence_rows = seg_row.shape[0]
    kv_local = key_matrix.shape[1] // HEAD_SIZE
    heads_local = w_query.shape[1] // HEAD_SIZE
    query_groups = heads_local // kv_local
    experts_win = w_gate.shape[0]
    block_rows = min(512, sequence_rows)
    scale_factor = HEAD_SIZE ** (-0.5)
    cosine_table, sine_values = rotary_tables(sequence_rows)
    rows_in = hidden_in.astype(jnp.float32)
    attention_normed, unit_attn, inverse_attn = norm_forward(rows_in, gain_attn)
    gathered = lax.all_gather(
        jnp.concatenate([attention_normed, cotangent], axis=1), "tensor", axis=0, tiled=True
    )
    full_attn = gathered[:, :width]
    grad_full = gathered[:, width:]
    query_before_rotary = jnp.dot(full_attn, w_query, preferred_element_type=jnp.float32).reshape(
        sequence_rows, heads_local, HEAD_SIZE
    )
    key_before_rotary = jnp.dot(full_attn, key_matrix, preferred_element_type=jnp.float32).reshape(
        sequence_rows, kv_local, HEAD_SIZE
    )
    query_rows = (
        apply_rotary(query_before_rotary, cosine_table, sine_values, 1.0)
        .astype(jnp.bfloat16)
        .reshape(sequence_rows, kv_local, query_groups, HEAD_SIZE)
    )
    keys_rot = apply_rotary(key_before_rotary, cosine_table, sine_values, 1.0).astype(jnp.bfloat16)
    value_inputs = (
        jnp.dot(full_attn, value_matrix, preferred_element_type=jnp.float32)
        .astype(jnp.bfloat16)
        .reshape(sequence_rows, kv_local, HEAD_SIZE)
    )
    row_start = 0
    row_stop = row_start + block_rows
    scores = block_scores(query_rows, keys_rot, seg_row, row_start, row_stop)
    peak_score = jnp.max(scores, axis=-1, keepdims=True)
    log_total = peak_score + jnp.log(jnp.sum(jnp.exp(scores - peak_score), axis=-1, keepdims=True))
    probs_blk = jnp.exp(scores - log_total)
    mixed_parts = jnp.einsum(
        "hgqk,khd->qhgd",
        probs_blk.astype(jnp.bfloat16),
        value_inputs,
        preferred_element_type=jnp.float32,
    ).astype(jnp.bfloat16)
    log_totals = [log_total]
    mixed_flat = mixed_parts.reshape(sequence_rows, heads_local * HEAD_SIZE)
    attn_out = scatter_sum(
        jnp.dot(mixed_flat, attention_output_weight, preferred_element_type=jnp.float32)
    )
    after_attn = rows_in + attn_out
    normed_ffn, unit_ffn, inverse_ffn = norm_forward(after_attn, gain_ffn)
    router_logits = jnp.dot(normed_ffn, w_router, preferred_element_type=jnp.float32)
    router_probs = jax.nn.softmax(router_logits, axis=-1)
    picked_mask = (routes[:, :, None] == jnp.arange(experts_win)[None, None, :]).astype(jnp.float32)
    route_counts = jnp.sum(picked_mask, axis=1)
    combine_bf = (router_probs[:, :experts_win] * route_counts).astype(jnp.bfloat16)
    gathered_ffn = lax.all_gather(beside(normed_ffn, combine_bf), "tensor", axis=0, tiled=True)
    full_ffn = gathered_ffn[:, :width]
    full_combine = gathered_ffn[:, width : width + experts_win]
    combine_used = full_combine.astype(jnp.float32)
    combined = jnp.zeros((sequence_rows, width), jnp.float32)
    saved_parts = []
    for expert in range(experts_win):
        gate_pre = jnp.dot(full_ffn, w_gate[expert], preferred_element_type=jnp.float32)
        up_pre = jnp.dot(full_ffn, w_up[expert], preferred_element_type=jnp.float32)
        silu_val, slope_val = gate_parts(gate_pre)
        inner_act = (silu_val * up_pre).astype(jnp.bfloat16)
        expert_out = jnp.dot(inner_act, w_down[expert], preferred_element_type=jnp.float32)
        combined = combined + combine_used[:, expert : expert + 1] * expert_out
        saved_parts.append((up_pre, silu_val, slope_val, inner_act, expert_out))
    combined = combined.astype(jnp.bfloat16)
    grad_full32 = grad_full.astype(jnp.float32)
    partial_rows = jnp.zeros((sequence_rows, width), jnp.float32)
    grad_combine_list, grad_gate_list, grad_up_list, grad_down_list = ([], [], [], [])
    for expert in range(experts_win):
        up_pre, silu_val, slope_val, inner_act, expert_out = saved_parts[expert]
        grad_expert = (combine_used[:, expert : expert + 1] * grad_full32).astype(jnp.bfloat16)
        grad_combine_list.append(jnp.sum(grad_full32 * expert_out, axis=-1))
        grad_down_list.append(inner_rows(inner_act, grad_expert))
        grad_inner = outer_columns(grad_expert, w_down[expert])
        grad_gate_pre = (grad_inner * up_pre * slope_val).astype(jnp.bfloat16)
        grad_up_pre = (grad_inner * silu_val).astype(jnp.bfloat16)
        grad_gate_list.append(grad_gate_pre)
        grad_up_list.append(grad_up_pre)
        partial_rows = (
            partial_rows
            + outer_columns(grad_gate_pre, w_gate[expert])
            + outer_columns(grad_up_pre, w_up[expert])
        )
    grad_combine_part = jnp.stack(grad_combine_list, axis=1)
    scattered = scatter_sum(beside(partial_rows.astype(jnp.bfloat16), grad_combine_part))
    grad_normed_part = scattered[:, :width]
    grad_combine = scattered[:, width : width + experts_win]
    grad_down = jnp.concatenate(grad_down_list, axis=0)
    grad_rprobs = jnp.concatenate(
        [
            grad_combine * route_counts,
            jnp.zeros((shard_rows, w_router.shape[1] - experts_win), jnp.float32),
        ],
        axis=1,
    )
    grad_logits = (
        router_probs * (grad_rprobs - jnp.sum(router_probs * grad_rprobs, axis=-1, keepdims=True))
    ).astype(jnp.bfloat16)
    grad_normed_ffn = grad_normed_part + outer_columns(grad_logits, w_router)
    grad_after, grad_gain_ffn = norm_backward(grad_normed_ffn, unit_ffn, inverse_ffn, gain_ffn)
    grad_after = grad_after + cotangent.astype(jnp.float32)
    gathered_after = lax.all_gather(
        beside(grad_after.astype(jnp.bfloat16), grad_logits), "tensor", axis=0, tiled=True
    )
    full_grad_after = gathered_after[:, :width]
    full_logits = gathered_after[:, width:]
    ffn_sums = inner_rows(
        full_ffn, jnp.concatenate(grad_gate_list + grad_up_list + [full_logits], axis=1)
    ).astype(jnp.bfloat16)
    grad_w_out = inner_rows(mixed_flat, full_grad_after)
    mixed_gradient = (
        outer_columns(full_grad_after, attention_output_weight)
        .astype(jnp.bfloat16)
        .reshape(sequence_rows, kv_local, query_groups, HEAD_SIZE)
    )
    delta_rows = jnp.transpose(
        jnp.sum(mixed_gradient.astype(jnp.float32) * mixed_parts.astype(jnp.float32), axis=-1),
        (1, 2, 0),
    )[..., None]
    grad_keys = jnp.zeros((sequence_rows, kv_local, HEAD_SIZE), jnp.float32)
    value_gradients = jnp.zeros((sequence_rows, kv_local, HEAD_SIZE), jnp.float32)
    grad_query_parts = []
    for block_index, row_start in enumerate(range(0, sequence_rows, block_rows)):
        row_stop = row_start + block_rows
        scores = block_scores(query_rows, keys_rot, seg_row, row_start, row_stop)
        probs_blk = jnp.exp(scores - log_totals[block_index])
        value_gradients = value_gradients.at[:row_stop].add(
            jnp.einsum(
                "hgqk,qhgd->khd",
                probs_blk.astype(jnp.bfloat16),
                mixed_gradient,
                preferred_element_type=jnp.float32,
            )
        )
        grad_probs = jnp.einsum(
            "qhgd,khd->hgqk", mixed_gradient, value_inputs, preferred_element_type=jnp.float32
        )
        grad_scores = (probs_blk * (grad_probs - delta_rows) * scale_factor).astype(jnp.bfloat16)
        grad_query_parts.append(
            jnp.einsum("hgqk,khd->qhgd", grad_scores, keys_rot, preferred_element_type=jnp.float32)
        )
        grad_keys = grad_keys.at[:row_stop].add(
            jnp.einsum(
                "hgqk,qhgd->khd", grad_scores, query_rows, preferred_element_type=jnp.float32
            )
        )
    grad_query = grad_query_parts[0].reshape(sequence_rows, heads_local, HEAD_SIZE)
    grad_query_bf = (
        apply_rotary(grad_query, cosine_table, sine_values, -1.0)
        .astype(jnp.bfloat16)
        .reshape(sequence_rows, heads_local * HEAD_SIZE)
    )
    key_gradient_half = (
        apply_rotary(grad_keys, cosine_table, sine_values, -1.0)
        .astype(jnp.bfloat16)
        .reshape(sequence_rows, kv_local * HEAD_SIZE)
    )
    value_gradient_half = value_gradients.astype(jnp.bfloat16).reshape(
        sequence_rows, kv_local * HEAD_SIZE
    )
    attn_sums = inner_rows(
        full_attn,
        jnp.concatenate([grad_query_bf, key_gradient_half, value_gradient_half], axis=1),
    ).astype(jnp.bfloat16)
    row_sums = jnp.concatenate([grad_down, grad_w_out], axis=0).astype(jnp.bfloat16)
    grad_normed_attn = scatter_sum(
        outer_columns(grad_query_bf, w_query)
        + outer_columns(key_gradient_half, key_matrix)
        + outer_columns(value_gradient_half, value_matrix)
    )
    grad_normed_attn, combined = lax.optimization_barrier((grad_normed_attn, combined))
    output = (after_attn + scatter_sum(combined)).astype(jnp.bfloat16)
    grad_in, grad_gain_attn = norm_backward(grad_normed_attn, unit_attn, inverse_attn, gain_attn)
    grad_in = grad_in + grad_after
    gains = jnp.concatenate([grad_gain_ffn, grad_gain_attn]).reshape(-1, 128)
    (
        grad_gate,
        grad_up,
        grad_router,
        grad_down,
        grad_w_out,
        grad_w_query,
        grad_w_key,
        grad_w_value,
        gains,
    ) = reduce_sums(
        ffn_sums, row_sums, attn_sums, gains, w_gate.shape, w_down.shape, w_query.shape, key_matrix.shape
    )
    gains = gains.reshape(2, width)
    grad_gain_ffn, grad_gain_attn = gains[0], gains[1]
    grad_router = grad_router[:, : w_router.shape[1]]
    grad_down = grad_down.reshape(w_down.shape)
    return (
        output,
        grad_in,
        grad_gain_attn,
        grad_w_query,
        grad_w_key,
        grad_w_value,
        grad_w_out,
        grad_gain_ffn,
        grad_router,
        grad_gate,
        grad_up,
        grad_down,
    )


def solution(mesh):
    return jax.shard_map(
        on_device,
        mesh=mesh,
        in_specs=(
            P(("dp", "tensor"), None),
            P(("dp", "tensor"), None),
            P("dp", None),
            P(("dp", "tensor"), None),
            P(),
            P(None, "tensor"),
            P(None, "tensor"),
            P(None, "tensor"),
            P("tensor", None),
            P(),
            P(),
            P(None, None, "tensor"),
            P(None, None, "tensor"),
            P(None, "tensor", None),
        ),
        out_specs=(
            P(("dp", "tensor"), None),
            P(("dp", "tensor"), None),
            P(),
            P(None, "tensor"),
            P(None, "tensor"),
            P(None, "tensor"),
            P("tensor", None),
            P(),
            P(),
            P(None, None, "tensor"),
            P(None, None, "tensor"),
            P(None, "tensor", None),
        ),
        check_vma=False,
    )
```
